1024 devices in a mesh: dp: 16 (over x_lo, y, core), seq: 64 (over z, x_hi).
Axes of the slice: x: 4 (x_hi: 2, x_lo: 2; x = x_hi * 2 + x_lo), y: 4, z: 32, core: 2. Of those that a mesh axis runs over, the one named last changes fastest.
Arguments:
- tokens: bfloat16 [131072, 1024], P(('dp', 'seq')), may hold values from -6 to 6
- gate_values: float32 [131072, 2], P(('dp', 'seq')), may hold values from 0.2 to 1
- expert_ids: int32 [131072, 2], P(('dp', 'seq')), may hold values from 0 to 31, all different within a row; in each aligned block of 128 rows (0 to 127, 128 to 255, ...) at most 9 rows name the same one
- cotangent: bfloat16 [131072, 1024], P(('dp', 'seq')), may hold values from -6 to 6
- weight_in: bfloat16 [32768, 1024], P('seq'), may hold values from -0.1875 to 0.1875
- weight_out: bfloat16 [32768, 1024], P('seq'), may hold values from -0.1875 to 0.1875
Outputs:
- layer_out: bfloat16 [131072, 1024], P(('dp', 'seq'))
- gate_grad: float32 [131072, 2], P(('dp', 'seq'))
- input_grad: bfloat16 [131072, 1024], P(('dp', 'seq'))
- weight_in_grad: float32 [1024, 32768], P('dp', 'seq')
- weight_out_grad: float32 [1024, 32768], P('dp', 'seq')
The draws below stay inside these ranges and needn't reach their ends.
Inputs may be any that keep to these rules, and one draw needn't show every extreme that they name: `expert_ids`: each row names two different experts; within the rows of one device no expert is named more than 9 times, a bound that some block reaches.
All inputs are finite; a program needn't handle non-finite values.
Results may differ from the reference program's by a relative error of at most 0.017.
Values may be sent and summed in bfloat16 or wider, within the bound.
A program may use at most 64 MiB of HBM per device.

```python
import math
import jax
import jax.numpy as jnp
import numpy as np
from jax import lax

D = 1024
E = 32
FF = 1024
TOK_DEV = 128
TOKENS = 131072
CAP = 9
BLOCK_UNITS = 512
BLOCKS = 2
N_DP = 16
N_SEQ = 64


def shard_levels(rng, dims, shards, low, top_value):
    level, own = 1.0, jax.random.fold_in(rng, 6)
    for position, blocks in shards:
        draws = jnp.exp(jax.random.uniform(jax.random.fold_in(own, position), (blocks,), jnp.float32, low / len(shards), top_value / len(shards)))
        level = level * jnp.repeat(draws, dims[position] // blocks).reshape([-1 if axis == position else 1 for axis in range(len(dims))])
    return level


def assign_block(stream_key, own, number, rows, amount, top, most, skew):
    order = jax.random.permutation(stream_key, amount)
    crowded, usual = portions_of(amount, rows * top, most, skew, True), portions_of(amount, rows * top, most, skew, False)
    places = jnp.arange(amount)

    def named(sizes, rotation):
        used = int((sizes > 0).sum())
        fixed = max(1, used // 4)
        passed = fixed + (places - fixed + rotation * (used - fixed)) % max(1, amount - fixed)
        return jnp.zeros((amount,), jnp.int32).at[order[jnp.where(places < fixed, places, passed)]].set(jnp.asarray(sizes, jnp.int32))

    sizes = jnp.where(number % 4 == 0, named(crowded, number // 4), named(usual, number - number // 4 - 1))
    mixed = jax.random.permutation(jax.random.fold_in(own, 3), amount)
    donor, taker = mixed[0:amount // 2 * 2:2], mixed[1:amount // 2 * 2:2]
    room = jnp.minimum(sizes[donor] - 1, most - sizes[taker]) // 2
    room = jnp.where((donor == order[0]) | (taker == order[0]) | (sizes[taker] == 0), 0, jnp.maximum(room, 0))
    passed = jax.random.randint(jax.random.fold_in(own, 4), (amount // 2,), 0, 1 << 20) % (room + 1)
    sizes = sizes.at[donor].add(-passed).at[taker].add(passed)
    labels = jnp.searchsorted(jnp.cumsum(sizes), jnp.arange(rows * top), side="right").astype(jnp.int32)
    listing = labels.reshape(top, rows).T
    listing = listing[jax.random.permutation(jax.random.fold_in(own, 1), rows)]
    rotation = jax.random.randint(jax.random.fold_in(own, 2), (rows, 1), 0, top)
    return jnp.take_along_axis(listing, (jnp.arange(top)[None, :] + rotation) % top, axis=1)


def portions_of(amount, total, limit, lean, full):
    weights = [(1 << 20) // math.isqrt(standing ** lean) + 1 for standing in range(1, amount + 1)]
    largest = limit if full else min(limit, max(-(-total // amount), total * weights[0] // sum(weights)))
    least = 1 if total - largest >= amount - 1 else 0
    counts, surplus = [largest] + [least] * (amount - 1), total - largest - least * (amount - 1)
    while surplus > 0:
        movable = [i for i in range(1, amount) if counts[i] < largest] or [i for i in range(1, amount) if counts[i] < limit]
        whole, remaining = sum([weights[i] for i in movable]), surplus
        for i in movable:
            more = min(limit - counts[i], max(1, remaining * weights[i] // whole), surplus)
            counts[i] = counts[i] + more
            surplus = surplus - more
    return np.array(counts)


def bell_draw(stream_key, shape, spread, bound, cuts=(), held_as=jnp.bfloat16):
    result = jax.random.normal(stream_key, shape, jnp.float32) * spread
    if len(cuts) > 0:
        result = shard_levels(stream_key, shape, cuts, -0.22, 0.18) * result
    return jnp.clip(result, min=-bound, max=bound).astype(held_as)


def setup_inputs(seed: int = 0) -> dict:
    seeds = jax.random.split(jax.random.key(seed), 7)
    tokens = bell_draw(seeds[0], (TOKENS, D), 1.0, 6.0, ((0, 1024),))
    gate_values = jnp.clip(0.2 + 0.8 * jax.random.uniform(seeds[1], (TOKENS, 2), jnp.float32) ** shard_levels(seeds[1], (TOKENS, 2), ((0, 1024),), -0.2, 0.2), 0.2, 1.0)
    expert_ids_keys = jax.random.split(jax.random.fold_in(seeds[2], 1), TOKENS // TOK_DEV)
    expert_ids_turns = jax.random.permutation(jax.random.fold_in(seeds[2], 3), TOKENS // TOK_DEV)
    expert_ids = jax.vmap(lambda own, number: assign_block(jax.random.fold_in(seeds[2], 2), own, number, TOK_DEV, E, 2, CAP, 2))(expert_ids_keys, expert_ids_turns).reshape((TOKENS, 2))
    cotangent = bell_draw(seeds[3], (TOKENS, D), 1.0, 6.0, ((0, 1024),))
    weight_in = bell_draw(seeds[4], (E * FF, D), D ** -0.5, 0.1875, ((0, 64),))
    weight_out = bell_draw(seeds[5], (E * FF, D), FF ** -0.5, 0.1875, ((0, 64),))
    return {"tokens": tokens, "gate_values": gate_values, "expert_ids": expert_ids, "cotangent": cotangent, "weight_in": weight_in, "weight_out": weight_out}


gelu_scale = 0.7978845608028654
gelu_cubic = 0.044715


def gelu_value(values):
    inner_arg = gelu_scale * (values + gelu_cubic * values * values * values)
    return 0.5 * values * (1.0 + jnp.tanh(inner_arg))


def gelu_slope(values):
    inner_arg = gelu_scale * (values + gelu_cubic * values * values * values)
    tanh_val = jnp.tanh(inner_arg)
    return 0.5 * (1.0 + tanh_val) + 0.5 * values * (1.0 - tanh_val * tanh_val) * gelu_scale * (1.0 + 3.0 * gelu_cubic * values * values)


def slot_numbers(ids_block):
    flat_ids = ids_block.reshape(-1)
    onehot = (flat_ids[:, None] == jnp.arange(E, dtype=jnp.int32)[None, :]).astype(jnp.int32)
    before = jnp.cumsum(onehot, axis=0) - onehot
    return jnp.sum(before * onehot, axis=1).reshape(ids_block.shape).astype(jnp.int32)


def fill_block(target_block, token_block, gate_block, cot_block):
    flat_target = target_block.reshape(-1)
    token_of = jnp.repeat(jnp.arange(TOK_DEV, dtype=jnp.int32), 2)
    slot_token = jnp.zeros((E * CAP,), jnp.int32).at[flat_target].set(token_of)
    slot_used = jnp.zeros((E * CAP,), jnp.float32).at[flat_target].set(1.0)
    slot_gate = jnp.zeros((E * CAP,), jnp.float32).at[flat_target].set(gate_block.reshape(-1))
    x_rows = (token_block[slot_token].astype(jnp.float32) * slot_used[:, None]).astype(jnp.bfloat16)
    d_rows = (cot_block[slot_token].astype(jnp.float32) * slot_gate[:, None]).astype(jnp.bfloat16)
    return x_rows, d_rows


def reference(tokens, gate_values, expert_ids, cotangent, weight_in, weight_out):
    factor = (E / (2.0 * TOKENS)) ** 0.5
    rows_group = N_SEQ * CAP
    win_all = weight_in.reshape(E, FF, D).astype(jnp.float32)
    wout_all = weight_out.reshape(E, FF, D).astype(jnp.float32)
    win_blocks = win_all.reshape(E, BLOCKS, BLOCK_UNITS, D)
    wout_blocks = wout_all.reshape(E, BLOCKS, BLOCK_UNITS, D)

    def one_group(carry, group_data):
        tok_group, gate_group, ids_group, cot_group = group_data
        slot_of = jax.vmap(slot_numbers)(ids_group)
        target = ids_group * CAP + slot_of
        x_buf, d_buf = jax.vmap(fill_block)(target, tok_group, gate_group, cot_group)
        x_buf = x_buf.reshape(N_SEQ, E, CAP, D).transpose(1, 0, 2, 3).reshape(E, rows_group, D)
        d_buf = d_buf.reshape(N_SEQ, E, CAP, D).transpose(1, 0, 2, 3).reshape(E, rows_group, D)
        x_float = x_buf.astype(jnp.float32)
        d_float = d_buf.astype(jnp.float32)
        hidden = jnp.einsum('erd,efd->erf', x_float, win_all)
        act = gelu_value(hidden).astype(jnp.bfloat16)
        act_float = act.astype(jnp.float32)
        part_out = jnp.einsum('erbh,ebhd->erbd', act_float.reshape(E, rows_group, BLOCKS, BLOCK_UNITS), wout_blocks).astype(jnp.bfloat16)
        back_hidden = jnp.einsum('erd,efd->erf', d_float, wout_all)
        dhid = (back_hidden * gelu_slope(hidden)).astype(jnp.bfloat16)
        dhid_float = dhid.astype(jnp.float32)
        part_in = jnp.einsum('erbh,ebhd->erbd', dhid_float.reshape(E, rows_group, BLOCKS, BLOCK_UNITS), win_blocks).astype(jnp.bfloat16)
        grad_out_group = (jnp.einsum('erd,erf->edf', d_float, act_float) * factor).astype(jnp.bfloat16)
        grad_in_group = (jnp.einsum('erd,erf->edf', x_float, dhid_float) * factor).astype(jnp.bfloat16)
        seq_index = jnp.arange(N_SEQ, dtype=jnp.int32)[:, None, None]
        rows_at = seq_index * CAP + slot_of
        expert_out = jnp.sum(part_out[ids_group, rows_at].astype(jnp.float32), axis=3)
        layer_part = jnp.sum(gate_group[..., None] * expert_out, axis=2).astype(jnp.bfloat16)
        gate_part = jnp.sum(cot_group.astype(jnp.float32)[:, :, None, :] * expert_out, axis=3)
        input_part = jnp.sum(part_in[ids_group, rows_at].astype(jnp.float32), axis=(2, 3)).astype(jnp.bfloat16)
        new_carry = (carry[0] + grad_in_group.astype(jnp.float32), carry[1] + grad_out_group.astype(jnp.float32))
        return new_carry, (layer_part, gate_part, input_part)

    group_data = (tokens.reshape(N_DP, N_SEQ, TOK_DEV, D), gate_values.reshape(N_DP, N_SEQ, TOK_DEV, 2),
                  expert_ids.reshape(N_DP, N_SEQ, TOK_DEV, 2), cotangent.reshape(N_DP, N_SEQ, TOK_DEV, D))
    start_carry = (jnp.zeros((E, D, FF), jnp.float32), jnp.zeros((E, D, FF), jnp.float32))
    final_carry, stacked = lax.scan(one_group, start_carry, group_data)
    layer_out = stacked[0].reshape(TOKENS, D)
    gate_grad = stacked[1].reshape(TOKENS, 2)
    input_grad = stacked[2].reshape(TOKENS, D)
    weight_in_grad = final_carry[0].transpose(1, 0, 2).reshape(D, E * FF)
    weight_out_grad = final_carry[1].transpose(1, 0, 2).reshape(D, E * FF)
    return layer_out, gate_grad, input_grad, weight_in_grad, weight_out_grad
```

```python
import functools

import jax
import jax.numpy as jnp
from jax import lax
from jax.experimental import pallas as pl
from jax.experimental.pallas import tpu as pltpu
from jax.sharding import PartitionSpec as P

MESH = pl.DeviceIdType.MESH
BF16 = jnp.bfloat16
F32 = jnp.float32

D = 1024
E = 32
FF = 1024
CAP = 9
TOK = 128
ROWS = E * CAP
PLANES = 32
SLAB = 32
FCHUNK = 256

gelu_scale = 0.7978845608028654
gelu_cubic = 0.044715

VMEM = pl.BlockSpec(memory_space=pltpu.VMEM)


def plane_device(expert, plane):
    return {
        "dp": (expert % 8) // 4 * 8 + expert % 4 * 2 + expert // 16,
        "seq": plane * 2 + (expert % 16) // 8,
    }


def position():
    seq = lax.axis_index("seq")
    dp = lax.axis_index("dp")
    plane = seq // 2
    x_hi = seq % 2
    own = x_hi * 8 + dp // 8 * 4 + (dp // 2) % 4 + 16 * (dp % 2)
    return plane, x_hi, dp, own


def up_of(plane, x_hi):
    return {"seq": (plane + 1) % PLANES * 2 + x_hi}


def down_of(plane, x_hi):
    return {"seq": (plane + PLANES - 1) % PLANES * 2 + x_hi}


def enter(plane, x_hi, own):
    barrier = pltpu.get_barrier_semaphore()
    pl.semaphore_signal(barrier, inc=1, device_id=up_of(plane, x_hi), device_id_type=MESH)
    pl.semaphore_signal(barrier, inc=1, device_id=down_of(plane, x_hi), device_id_type=MESH)

    @pl.loop(1, E)
    def _(k):
        pl.semaphore_signal(
            barrier, inc=1, device_id=plane_device((own + k) % E, plane), device_id_type=MESH
        )

    pl.semaphore_wait(barrier, E + 1)


def dot_t(a, b):
    return lax.dot_general(a, b, (((1,), (1,)), ((), ())), preferred_element_type=F32)


def dot_cols(a, b):
    return lax.dot_general(a, b, (((0,), (0,)), ((), ())), preferred_element_type=F32)


def pick_kernel(ids_ref, gate_ref, tok_ref, cot_ref, send_ref, pos_ref):
    expert = lax.broadcasted_iota(jnp.int32, (E, TOK), 0)
    hot = [(expert == ids_ref[k : k + 1, :]).astype(F32) for k in range(2)]
    row = lax.broadcasted_iota(jnp.int32, (TOK, TOK), 0)
    col = lax.broadcasted_iota(jnp.int32, (TOK, TOK), 1)
    earlier = (row < col).astype(BF16)
    before = jnp.dot((hot[0] + hot[1]).astype(BF16), earlier, preferred_element_type=F32)
    slot_row = lax.broadcasted_iota(jnp.int32, (ROWS, TOK), 0)
    picks = []
    gates = jnp.zeros((ROWS, 1), F32)
    for k in range(2):
        slot = jnp.sum(before * hot[k], axis=0, keepdims=True).astype(jnp.int32)
        at = ids_ref[k : k + 1, :] * CAP + slot
        pos_ref[k : k + 1, :] = at
        pick = slot_row == at
        picks.append(pick)
        gates = gates + jnp.sum(
            jnp.where(pick, gate_ref[k : k + 1, :], 0.0), axis=1, keepdims=True
        )
    both = (picks[0] | picks[1]).astype(F32).astype(BF16)
    x_rows = jnp.dot(both, tok_ref[...], preferred_element_type=F32).astype(BF16)
    send_ref[:, 0:CAP] = x_rows.reshape(ROWS, 8, 128).reshape(E, CAP, 8, 128)
    d_rows = (jnp.dot(both, cot_ref[...], preferred_element_type=F32) * gates).astype(BF16)
    send_ref[:, CAP : 2 * CAP] = d_rows.reshape(ROWS, 8, 128).reshape(E, CAP, 8, 128)


def start_rows(plane, own, src, dst, ssem, rsem):
    keep = pltpu.make_async_copy(src.at[own], dst.at[own], ssem.at[0])
    keep.start()

    def copy(k):
        to = (own + k) % E
        return pltpu.make_async_remote_copy(
            src_ref=src.at[to],
            dst_ref=dst.at[own],
            send_sem=ssem.at[k],
            recv_sem=rsem.at[k],
            device_id=plane_device(to, plane),
            device_id_type=MESH,
        )

    @pl.loop(1, E)
    def _(k):
        copy(k).start()

    def finish():
        keep.wait()

        @pl.loop(1, E)
        def _(k):
            copy(k).wait()

    return finish


def gather_kernel(
    send_ref, win_ref, wout_ref, rows_ref, fin_ref, fout_ref,
    held, own_sem, tok_send, tok_recv, ring_send, ring_recv, host_send, host_recv,
):
    plane, x_hi, dp, own = position()
    up, down = up_of(plane, x_hi), down_of(plane, x_hi)
    slab = pl.ds(pl.multiple_of(dp * SLAB, SLAB), SLAB)
    place = pl.ds(pl.multiple_of(x_hi * (FF // 2) + dp * SLAB, SLAB), SLAB)
    locals_ = [
        pltpu.make_async_copy(ref.at[slab], held.at[a, plane], own_sem.at[a])
        for a, ref in enumerate((win_ref, wout_ref))
    ]
    for c in locals_:
        c.start()
    enter(plane, x_hi, own)
    for c in locals_:
        c.wait()
    full = (fin_ref, fout_ref)

    def ring(direction, a, step):
        if direction == 0:
            e, to = (plane - (step - 1) + 2 * PLANES) % PLANES, up
        else:
            e, to = (plane + (step - 1)) % PLANES, down
        return pltpu.make_async_remote_copy(
            src_ref=held.at[a, e],
            dst_ref=held.at[a, e],
            send_sem=ring_send.at[direction, a, step],
            recv_sem=ring_recv.at[direction, a, step],
            device_id=to,
            device_id_type=MESH,
        )

    def arrival(direction, a, step):
        e = (plane - step + 2 * PLANES) % PLANES if direction == 0 else (plane + step) % PLANES
        to = up if direction == 0 else down
        return pltpu.make_async_remote_copy(
            src_ref=held.at[a, e],
            dst_ref=held.at[a, e],
            send_sem=ring_send.at[direction, a, step],
            recv_sem=ring_recv.at[direction, a, step],
            device_id=to,
            device_id_type=MESH,
        )

    def to_host(a, e):
        return pltpu.make_async_remote_copy(
            src_ref=held.at[a, e],
            dst_ref=full[a].at[place],
            send_sem=host_send.at[a, e],
            recv_sem=host_recv.at[a, own],
            device_id=plane_device(e, plane),
            device_id_type=MESH,
        )

    def to_self(a, e):
        return pltpu.make_async_copy(held.at[a, e], full[a].at[place], host_recv.at[a, own])

    def deliver(e):
        for a in range(2):
            @pl.when(e == own)
            def _():
                to_self(a, e).start()

            @pl.when(e != own)
            def _():
                to_host(a, e).start()

    for a in range(2):
        ring(0, a, 1).start()
        ring(1, a, 1).start()
    deliver(plane)
    finish_rows = start_rows(plane, own, send_ref, rows_ref, tok_send, tok_recv)

    @pl.loop(1, 17)
    def _(step):
        for a in range(2):
            arrival(0, a, step).wait_recv()

            @pl.when(step < 16)
            def _():
                ring(0, a, step + 1).start()

            @pl.when(step < 16)
            def _():
                arrival(1, a, step).wait_recv()

            @pl.when(step < 15)
            def _():
                ring(1, a, step + 1).start()

        @pl.when(step % 4 == 0)
        def _():
            @pl.loop(0, 8)
            def _(i):
                j = (i + own) % 8
                away = step - 3 + j // 2

                @pl.when(j % 2 == 0)
                def _():
                    deliver((plane - away + 2 * PLANES) % PLANES)

                @pl.when((j % 2 == 1) & (away < 16))
                def _():
                    deliver((plane + away) % PLANES)

    finish_rows()

    @pl.loop(1, 17)
    def _(step):
        for a in range(2):
            ring(0, a, step).wait_send()

            @pl.when(step < 16)
            def _():
                ring(1, a, step).wait_send()

    @pl.loop(0, E)
    def _(e):
        there = pl.ds(
            pl.multiple_of((e % 16) // 8 * (FF // 2) + ((e % 8) // 4 * 8 + e % 4 * 2 + e // 16) * SLAB, SLAB),
            SLAB,
        )
        for a in range(2):
            @pl.when(e != own)
            def _():
                to_host(a, e).wait_send()

            pltpu.make_async_copy(held.at[a, e], full[a].at[there], host_recv.at[a, e]).wait()


def expert_kernel(factor, rows_ref, fin_ref, fout_ref, back_ref, grad_ref, x, d, out, inp):
    x[...] = rows_ref[:, 0:CAP].reshape(ROWS, 8, 128).reshape(ROWS, D)
    d[...] = rows_ref[:, CAP : 2 * CAP].reshape(ROWS, 8, 128).reshape(ROWS, D)
    out[...] = jnp.zeros_like(out)
    inp[...] = jnp.zeros_like(inp)

    @pl.loop(0, FF // FCHUNK)
    def _(c):
        units = pl.ds(pl.multiple_of(c * FCHUNK, FCHUNK), FCHUNK)
        wi = fin_ref[units, :]
        wo = fout_ref[units, :]
        v = dot_t(x[...], wi)
        t = jnp.tanh(gelu_scale * (v + gelu_cubic * v * v * v))
        act = (0.5 * v * (1.0 + t)).astype(BF16)
        slope = 0.5 * (1.0 + t) + 0.5 * v * (1.0 - t * t) * gelu_scale * (
            1.0 + 3.0 * gelu_cubic * v * v
        )
        dhid = (dot_t(d[...], wo) * slope).astype(BF16)
        out[...] += jnp.dot(act, wo, preferred_element_type=F32)
        inp[...] += jnp.dot(dhid, wi, preferred_element_type=F32)
        cols = pl.ds(pl.multiple_of(c % 2 * FCHUNK, FCHUNK), FCHUNK)
        g_in = (dot_cols(x[...], dhid) * factor).astype(BF16)
        grad_ref[c // 2, :, 0, :, cols] = g_in.reshape(16, 64, FCHUNK)
        g_out = (dot_cols(d[...], act) * factor).astype(BF16)
        grad_ref[c // 2, :, 1, :, cols] = g_out.reshape(16, 64, FCHUNK)

    back_ref[:, 0:CAP] = out[...].astype(BF16).reshape(ROWS, 8, 128).reshape(E, CAP, 8, 128)
    back_ref[:, CAP : 2 * CAP] = inp[...].astype(BF16).reshape(ROWS, 8, 128).reshape(E, CAP, 8, 128)


def scatter_kernel(
    back_ref, grad_ref, rows_ref, gin_ref, gout_ref,
    parts, up_got, up_held, down_got, down_held,
    tok_send, tok_recv, part_send, part_recv, up_send, up_recv, down_send, down_recv,
):
    plane, x_hi, dp, own = position()
    up, down = up_of(plane, x_hi), down_of(plane, x_hi)
    enter(plane, x_hi, own)

    def part(k):
        to = (own + k) % E
        dev = plane_device(to, plane)
        return pltpu.make_async_remote_copy(
            src_ref=grad_ref.at[(to % 16) // 8, dev["dp"]],
            dst_ref=parts.at[own],
            send_sem=part_send.at[k],
            recv_sem=part_recv.at[own],
            device_id=dev,
            device_id_type=MESH,
        )

    def own_part():
        return pltpu.make_async_copy(grad_ref.at[x_hi, dp], parts.at[own], part_recv.at[own])

    at_up = (plane + 16 - own + PLANES) % PLANES
    my_step = jnp.where(at_up < 16, at_up, 31 - at_up)

    def send_parts(window):
        @pl.when(my_step // 4 == window)
        def _():
            own_part().start()

            @pl.loop(1, E)
            def _(k):
                part(k).start()

    def await_part(e):
        pltpu.make_async_copy(grad_ref.at[x_hi, dp], parts.at[e], part_recv.at[e]).wait()

    def up_copy(a, step, first=False):
        e = (plane + 16) % PLANES
        return pltpu.make_async_remote_copy(
            src_ref=parts.at[e, a] if first else up_held.at[step, a],
            dst_ref=up_got.at[step, a],
            send_sem=up_send.at[a, step],
            recv_sem=up_recv.at[a, step],
            device_id=up,
            device_id_type=MESH,
        )

    def down_copy(a, step, first=False):
        e = (plane - 15 + PLANES) % PLANES
        return pltpu.make_async_remote_copy(
            src_ref=parts.at[e, a] if first else down_held.at[step, a],
            dst_ref=down_got.at[step, a],
            send_sem=down_send.at[a, step],
            recv_sem=down_recv.at[a, step],
            device_id=down,
            device_id_type=MESH,
        )

    send_parts(0)
    send_parts(1)
    finish_rows = start_rows(plane, own, back_ref, rows_ref, tok_send, tok_recv)
    await_part((plane + 16) % PLANES)
    await_part((plane - 15 + PLANES) % PLANES)
    for a in range(2):
        up_copy(a, 0, True).start()
        down_copy(a, 0, True).start()

    @pl.loop(1, 16)
    def _(t):
        @pl.when(t == 4)
        def _():
            send_parts(2)

        @pl.when(t == 8)
        def _():
            send_parts(3)

        eu = (plane + 16 - t) % PLANES
        ed = (plane - 15 + t + PLANES) % PLANES
        await_part(eu)

        @pl.when(t < 15)
        def _():
            await_part(ed)

        for a in range(2):
            up_copy(a, t - 1).wait_recv()
            up_held[t, a] = (up_got[t - 1, a].astype(F32) + parts[eu, a].astype(F32)).astype(BF16)
            up_copy(a, t).start()

            @pl.when(t < 15)
            def _():
                down_copy(a, t - 1).wait_recv()
                down_held[t, a] = (
                    down_got[t - 1, a].astype(F32) + parts[ed, a].astype(F32)
                ).astype(BF16)
                down_copy(a, t).start()

    await_part(plane)
    for a, ref in enumerate((gin_ref, gout_ref)):
        up_copy(a, 15).wait_recv()
        down_copy(a, 14).wait_recv()
        ref[...] = (
            up_got[15, a].astype(F32) + down_got[14, a].astype(F32) + parts[plane, a].astype(F32)
        )
    finish_rows()

    @pl.loop(1, E)
    def _(k):
        part(k).wait_send()

    for a in range(2):
        up_copy(a, 0, True).wait_send()
        down_copy(a, 0, True).wait_send()

    @pl.loop(1, 16)
    def _(t):
        for a in range(2):
            up_copy(a, t).wait_send()

            @pl.when(t < 15)
            def _():
                down_copy(a, t).wait_send()


def combine_kernel(rows_ref, pos_ref, gate_ref, cot_ref, layer_ref, ggrad_ref, igrad_ref):
    out_rows = rows_ref[:, 0:CAP].reshape(ROWS, 8, 128).reshape(ROWS, D)
    in_rows = rows_ref[:, CAP : 2 * CAP].reshape(ROWS, 8, 128).reshape(ROWS, D)
    slot_row = lax.broadcasted_iota(jnp.int32, (ROWS, TOK), 0)
    picks = [slot_row == pos_ref[k : k + 1, :] for k in range(2)]
    cot = cot_ref[...].astype(F32)
    layer = jnp.zeros((TOK, D), F32)
    for k in range(2):
        got = dot_cols(picks[k].astype(F32).astype(BF16), out_rows)
        layer = layer + gate_ref[:, k : k + 1] * got
        ggrad_ref[:, k : k + 1] = jnp.sum(cot * got, axis=1, keepdims=True)
    layer_ref[...] = layer.astype(BF16)
    both = (picks[0] | picks[1]).astype(F32).astype(BF16)
    igrad_ref[...] = dot_cols(both, in_rows).astype(BF16)


def local(tokens, gate_values, expert_ids, cotangent, weight_in, weight_out):
    tok_all = TOK * lax.axis_size("dp") * lax.axis_size("seq")
    factor = (E / (2.0 * tok_all)) ** 0.5
    shape = jax.ShapeDtypeStruct
    dma = pltpu.SemaphoreType.DMA
    rows_shape = shape((E, 2 * CAP, 8, 128), BF16)
    big = pltpu.CompilerParams(vmem_limit_bytes=60 << 20)
    send, pos = pl.pallas_call(
        pick_kernel,
        out_shape=(rows_shape, shape((2, TOK), jnp.int32)),
        in_specs=[VMEM] * 4,
        out_specs=(VMEM, VMEM),
        compiler_params=big,
    )(expert_ids.T, gate_values.T, tokens, cotangent)
    rows, full_in, full_out = pl.pallas_call(
        gather_kernel,
        out_shape=(rows_shape, shape((FF, D), BF16), shape((FF, D), BF16)),
        in_specs=[VMEM] * 3,
        out_specs=(VMEM,) * 3,
        scratch_shapes=[
            pltpu.VMEM((2, E, SLAB, D), BF16),
            dma((2,)), dma((E,)), dma((E,)),
            dma((2, 2, 17)), dma((2, 2, 17)), dma((2, E)), dma((2, E)),
        ],
        compiler_params=pltpu.CompilerParams(
            collective_id=0, has_side_effects=True, vmem_limit_bytes=60 << 20
        ),
    )(send, weight_in, weight_out)
    back, grads = pl.pallas_call(
        functools.partial(expert_kernel, factor),
        out_shape=(rows_shape, shape((2, 16, 2, 64, FF // 2), BF16)),
        in_specs=[VMEM] * 3,
        out_specs=(VMEM, VMEM),
        scratch_shapes=[
            pltpu.VMEM((ROWS, D), BF16), pltpu.VMEM((ROWS, D), BF16),
            pltpu.VMEM((ROWS, D), F32), pltpu.VMEM((ROWS, D), F32),
        ],
        compiler_params=big,
    )(rows, full_in, full_out)
    piece = (2, 64, FF // 2)
    returned, grad_in, grad_out = pl.pallas_call(
        scatter_kernel,
        out_shape=(rows_shape, shape((64, FF // 2), F32), shape((64, FF // 2), F32)),
        in_specs=[VMEM] * 2,
        out_specs=(VMEM,) * 3,
        scratch_shapes=[
            pltpu.VMEM((E,) + piece, BF16),
            pltpu.VMEM((16,) + piece, BF16), pltpu.VMEM((16,) + piece, BF16),
            pltpu.VMEM((16,) + piece, BF16), pltpu.VMEM((16,) + piece, BF16),
            dma((E,)), dma((E,)), dma((E,)), dma((E,)),
            dma((2, 16)), dma((2, 16)), dma((2, 16)), dma((2, 16)),
        ],
        compiler_params=pltpu.CompilerParams(
            collective_id=1, has_side_effects=True, vmem_limit_bytes=60 << 20
        ),
    )(back, grads)
    layer_out, gate_grad, input_grad = pl.pallas_call(
        combine_kernel,
        out_shape=(shape((TOK, D), BF16), shape((TOK, 2), F32), shape((TOK, D), BF16)),
        in_specs=[VMEM] * 4,
        out_specs=(VMEM,) * 3,
        compiler_params=big,
    )(returned, pos, gate_values, cotangent)
    return layer_out, gate_grad, input_grad, grad_in, grad_out


def solution(mesh):
    tok = P(("dp", "seq"), None)
    return jax.shard_map(
        local,
        mesh=mesh,
        in_specs=(tok, tok, tok, tok, P("seq", None), P("seq", None)),
        out_specs=(tok, tok, tok, P("dp", "seq"), P("dp", "seq")),
        check_vma=False,
    )
```

```python
import functools

import jax
import jax.numpy as jnp
from jax import lax
from jax.experimental import pallas as pl
from jax.experimental.pallas import tpu as pltpu
from jax.sharding import PartitionSpec as P

MESH = pl.DeviceIdType.MESH
BF16 = jnp.bfloat16
F32 = jnp.float32

D = 1024
E = 32
FF = 1024
CAP = 9
TOK = 128
ROWS = E * CAP
PLANES = 32
PAIR = 64
PIECES = 4
AHEAD = 8
LAG = 0
WIN = 1
FCHUNK = 256

gelu_scale = 0.7978845608028654
gelu_cubic = 0.044715

VMEM = pl.BlockSpec(memory_space=pltpu.VMEM)


def plane_device(expert, plane):
    x = expert % 4
    y = (expert // 4 + x) % 4
    return {"dp": x % 2 * 8 + y * 2 + expert // 16 % 2, "seq": plane * 2 + x // 2}


def position():
    seq = lax.axis_index("seq")
    dp = lax.axis_index("dp")
    plane = seq // 2
    x_hi = seq % 2
    x = x_hi * 2 + dp // 8
    own = x + (dp // 2 % 4 - x + 4) % 4 * 4 + 16 * (dp % 2)
    return plane, x_hi, dp, own


def up_of(plane, x_hi):
    return {"seq": (plane + 1) % PLANES * 2 + x_hi}


def down_of(plane, x_hi):
    return {"seq": (plane + PLANES - 1) % PLANES * 2 + x_hi}


def enter(plane, x_hi, own):
    barrier = pltpu.get_barrier_semaphore()
    pl.semaphore_signal(barrier, inc=1, device_id=up_of(plane, x_hi), device_id_type=MESH)
    pl.semaphore_signal(barrier, inc=1, device_id=down_of(plane, x_hi), device_id_type=MESH)

    @pl.loop(1, E)
    def _(k):
        pl.semaphore_signal(
            barrier, inc=1, device_id=plane_device((own + k) % E, plane), device_id_type=MESH
        )

    pl.semaphore_wait(barrier, E + 1)


def dot_t(a, b):
    return lax.dot_general(a, b, (((1,), (1,)), ((), ())), preferred_element_type=F32)


def dot_cols(a, b):
    return lax.dot_general(a, b, (((0,), (0,)), ((), ())), preferred_element_type=F32)


def pick_kernel(ids_ref, gate_ref, tok_ref, cot_ref, send_ref, pos_ref):
    expert = lax.broadcasted_iota(jnp.int32, (E, TOK), 0)
    hot = [(expert == ids_ref[k : k + 1, :]).astype(F32) for k in range(2)]
    row = lax.broadcasted_iota(jnp.int32, (TOK, TOK), 0)
    col = lax.broadcasted_iota(jnp.int32, (TOK, TOK), 1)
    earlier = (row < col).astype(BF16)
    before = jnp.dot((hot[0] + hot[1]).astype(BF16), earlier, preferred_element_type=F32)
    slot_row = lax.broadcasted_iota(jnp.int32, (ROWS, TOK), 0)
    picks = []
    gates = jnp.zeros((ROWS, 1), F32)
    for k in range(2):
        slot = jnp.sum(before * hot[k], axis=0, keepdims=True).astype(jnp.int32)
        at = ids_ref[k : k + 1, :] * CAP + slot
        pos_ref[k : k + 1, :] = at
        pick = slot_row == at
        picks.append(pick)
        gates = gates + jnp.sum(
            jnp.where(pick, gate_ref[k : k + 1, :], 0.0), axis=1, keepdims=True
        )
    both = (picks[0] | picks[1]).astype(F32).astype(BF16)
    x_rows = jnp.dot(both, tok_ref[...], preferred_element_type=F32).astype(BF16)
    send_ref[:, 0:CAP] = x_rows.reshape(ROWS, 8, 128).reshape(E, CAP, 8, 128)
    d_rows = (jnp.dot(both, cot_ref[...], preferred_element_type=F32) * gates).astype(BF16)
    send_ref[:, CAP : 2 * CAP] = d_rows.reshape(ROWS, 8, 128).reshape(E, CAP, 8, 128)


def start_rows(plane, own, src, dst, ssem, rsem):
    keep = pltpu.make_async_copy(src.at[own], dst.at[own], ssem.at[0])
    keep.start()

    def copy(k):
        to = (own + k) % E
        return pltpu.make_async_remote_copy(
            src_ref=src.at[to],
            dst_ref=dst.at[own],
            send_sem=ssem.at[k],
            recv_sem=rsem.at[k],
            device_id=plane_device(to, plane),
            device_id_type=MESH,
        )

    @pl.loop(1, E)
    def _(k):
        copy(k).start()

    def finish():
        keep.wait()

        @pl.loop(1, E)
        def _(k):
            copy(k).wait()

    return finish


def gather_kernel(
    send_ref, win_ref, wout_ref, rows_ref, fin_ref, fout_ref,
    held, own_sem, tok_send, tok_recv, ring_send, ring_recv, host_send, host_recv,
):
    plane, x_hi, dp, own = position()
    core = dp % 2
    chip = x_hi * 8 + dp // 2
    steps = 16 - core
    toward = 1 - 2 * core
    onward = {"seq": (plane + toward + PLANES) % PLANES * 2 + x_hi}
    slab = pl.ds(pl.multiple_of(dp // 2 * PAIR, PAIR), PAIR)
    place = pl.ds(pl.multiple_of(chip * PAIR, PAIR), PAIR)
    full = (fin_ref, fout_ref)
    mine = [
        pltpu.make_async_copy(ref.at[slab], held.at[a, 0], own_sem.at[a])
        for a, ref in enumerate((win_ref, wout_ref))
    ]
    for c in mine:
        c.start()
    enter(plane, x_hi, own)
    for c in mine:
        c.wait()
    cut = PAIR // PIECES

    def ring(a, h, step):
        return pltpu.make_async_remote_copy(
            src_ref=held.at[a, step - 1, pl.ds(h * cut, cut)],
            dst_ref=held.at[a, step, pl.ds(h * cut, cut)],
            send_sem=ring_send.at[a, h, step],
            recv_sem=ring_recv.at[a, h, step],
            device_id=onward,
            device_id_type=MESH,
        )

    def to_host(a, step):
        return pltpu.make_async_remote_copy(
            src_ref=held.at[a, step],
            dst_ref=full[a].at[place],
            send_sem=host_send.at[a, step],
            recv_sem=host_recv.at[a, chip],
            device_id=plane_device((plane - toward * step + 2 * PLANES) % PLANES, plane),
            device_id_type=MESH,
        )

    def is_own(step):
        return (plane - toward * step + 2 * PLANES) % PLANES == own

    def deliver(step):
        for a in range(2):
            @pl.when(is_own(step))
            def _():
                pltpu.make_async_copy(
                    held.at[a, step], full[a].at[place], host_recv.at[a, chip]
                ).start()

            @pl.when(~is_own(step))
            def _():
                to_host(a, step).start()

    for h in range(PIECES):
        for a in range(2):
            ring(a, h, 1).start()

    @pl.when(core == 1)
    def _():
        deliver(0)

    finish_rows = start_rows(plane, own, send_ref, rows_ref, tok_send, tok_recv)

    @pl.loop(1, 17)
    def _(step):
        @pl.when(step <= steps)
        def _():
            for h in range(PIECES):
                for a in range(2):
                    ring(a, h, step).wait_recv()

                    @pl.when(step < steps)
                    def _():
                        ring(a, h, step + 1).start()

        @pl.when(step % WIN == 0)
        def _():
            @pl.loop(0, WIN)
            def _(i):
                at = step - WIN + 1 + (i + own) % WIN

                @pl.when(at <= steps)
                def _():
                    deliver(at)

    finish_rows()

    @pl.loop(1, 17)
    def _(step):
        @pl.when(step <= steps)
        def _():
            for a in range(2):
                for h in range(PIECES):
                    ring(a, h, step).wait_send()

    @pl.loop(0, 17)
    def _(step):
        for a in range(2):
            @pl.when((step <= steps) & ((step > 0) | (core == 1)) & ~is_own(step))
            def _():
                to_host(a, step).wait_send()

    @pl.loop(0, 16)
    def _(c):
        there = pl.ds(pl.multiple_of(c * PAIR, PAIR), PAIR)
        for a in range(2):
            pltpu.make_async_copy(held.at[a, 0], full[a].at[there], host_recv.at[a, c]).wait()


def expert_kernel(factor, rows_ref, fin_ref, fout_ref, back_ref, grad_ref, x, d, out, inp):
    x[...] = rows_ref[:, 0:CAP].reshape(ROWS, 8, 128).reshape(ROWS, D)
    d[...] = rows_ref[:, CAP : 2 * CAP].reshape(ROWS, 8, 128).reshape(ROWS, D)
    out[...] = jnp.zeros_like(out)
    inp[...] = jnp.zeros_like(inp)

    @pl.loop(0, FF // FCHUNK)
    def _(c):
        units = pl.ds(pl.multiple_of(c * FCHUNK, FCHUNK), FCHUNK)
        wi = fin_ref[units, :]
        wo = fout_ref[units, :]
        v = dot_t(x[...], wi)
        t = jnp.tanh(gelu_scale * (v + gelu_cubic * v * v * v))
        act = (0.5 * v * (1.0 + t)).astype(BF16)
        slope = 0.5 * (1.0 + t) + 0.5 * v * (1.0 - t * t) * gelu_scale * (
            1.0 + 3.0 * gelu_cubic * v * v
        )
        dhid = (dot_t(d[...], wo) * slope).astype(BF16)
        out[...] += jnp.dot(act, wo, preferred_element_type=F32)
        inp[...] += jnp.dot(dhid, wi, preferred_element_type=F32)
        cols = pl.ds(pl.multiple_of(c % 2 * FCHUNK, FCHUNK), FCHUNK)
        g_in = (dot_cols(x[...], dhid) * factor).astype(BF16)
        grad_ref[c // 2, :, :, 0, :, cols] = g_in.reshape(8, PIECES, 128 // PIECES, FCHUNK)
        g_out = (dot_cols(d[...], act) * factor).astype(BF16)
        grad_ref[c // 2, :, :, 1, :, cols] = g_out.reshape(8, PIECES, 128 // PIECES, FCHUNK)

    back_ref[:, 0:CAP] = out[...].astype(BF16).reshape(ROWS, 8, 128).reshape(E, CAP, 8, 128)
    back_ref[:, CAP : 2 * CAP] = inp[...].astype(BF16).reshape(ROWS, 8, 128).reshape(E, CAP, 8, 128)


def scatter_kernel(
    back_ref, grad_ref, rows_ref, gin_ref, gout_ref,
    parts, got, held, other,
    tok_send, tok_recv, part_send, part_recv, ring_send, ring_recv, swap_send, swap_recv,
):
    plane, x_hi, dp, own = position()
    core = dp % 2
    chip = x_hi * 8 + dp // 2
    steps = 16 - core
    toward = 1 - 2 * core
    onward = {"seq": (plane + toward + PLANES) % PLANES * 2 + x_hi}
    cut = 2 * 64 // PIECES
    enter(plane, x_hi, own)

    at_up = (plane + 16 - own + PLANES) % PLANES
    goes_down = at_up // 17
    my_step = at_up + goes_down * (31 - 2 * at_up)

    def part(k, h):
        to = (chip + k) % 16
        return pltpu.make_async_remote_copy(
            src_ref=grad_ref.at[to // 8, to % 8, h],
            dst_ref=parts.at[my_step, h],
            send_sem=part_send.at[h, k],
            recv_sem=part_recv.at[h, my_step],
            device_id={"dp": to % 8 * 2 + goes_down, "seq": plane * 2 + to // 8},
            device_id_type=MESH,
        )

    def send_parts():
        @pl.loop(0, PIECES)
        def _(h):
            @pl.when(goes_down == core)
            def _():
                pltpu.make_async_copy(
                    grad_ref.at[x_hi, dp // 2, h], parts.at[my_step, h], part_recv.at[h, my_step]
                ).start()

            @pl.when(goes_down != core)
            def _():
                part(0, h).start()

            @pl.loop(1, 16)
            def _(k):
                part(k, h).start()

    def await_part(step, h):
        pltpu.make_async_copy(
            grad_ref.at[x_hi, dp // 2, h], parts.at[step, h], part_recv.at[h, step]
        ).wait()

    def ring(h, step, first=False):
        return pltpu.make_async_remote_copy(
            src_ref=parts.at[0, h] if first else held.at[step, h],
            dst_ref=got.at[step, h],
            send_sem=ring_send.at[h, step],
            recv_sem=ring_recv.at[h, step],
            device_id=onward,
            device_id_type=MESH,
        )

    @pl.when(my_step < AHEAD)
    def _():
        send_parts()

    finish_rows = start_rows(plane, own, back_ref, rows_ref, tok_send, tok_recv)

    @pl.loop(0, 16 + LAG * (PIECES - 1))
    def _(tick):
        @pl.when(my_step == tick + AHEAD)
        def _():
            send_parts()

        for h in range(PIECES):
            t = tick - LAG * h

            @pl.when(t == 0)
            def _():
                await_part(0, h)
                ring(h, 0, True).start()

            @pl.when((t > 0) & (t < steps))
            def _():
                await_part(t, h)
                ring(h, t - 1).wait_recv()
                held[t, h] = (got[t - 1, h].astype(F32) + parts[t, h].astype(F32)).astype(BF16)
                ring(h, t).start()

    @pl.when(my_step >= 16 + LAG * (PIECES - 1) + AHEAD)
    def _():
        send_parts()

    for h in range(PIECES):
        ring(h, steps - 1).wait_recv()

        @pl.when(core == 0)
        def _():
            await_part(16, h)
            held[0, h] = (got[15, h].astype(F32) + parts[16, h].astype(F32)).astype(BF16)

        @pl.when(core == 1)
        def _():
            held[0, h] = got[14, h]

    half = PIECES // 2
    mine = pl.ds(core * half, half)
    theirs = pl.ds(half - core * half, half)
    swap = pltpu.make_async_remote_copy(
        src_ref=held.at[0, theirs],
        dst_ref=other,
        send_sem=swap_send,
        recv_sem=swap_recv,
        device_id={"dp": dp + 1 - 2 * core},
        device_id_type=MESH,
    )
    swap.start()
    swap.wait()
    total = held[0, mine].astype(F32) + other[...].astype(F32)
    for a, ref in enumerate((gin_ref, gout_ref)):
        ref[...] = total[:, a].reshape(64, FF // 2)
    finish_rows()

    @pl.loop(0, PIECES)
    def _(h):
        @pl.when(goes_down != core)
        def _():
            part(0, h).wait_send()

        @pl.loop(1, 16)
        def _(k):
            part(k, h).wait_send()

    for h in range(PIECES):
        ring(h, 0, True).wait_send()

    @pl.loop(1, 16)
    def _(t):
        @pl.when(t < steps)
        def _():
            for h in range(PIECES):
                ring(h, t).wait_send()


def combine_kernel(rows_ref, pos_ref, gate_ref, cot_ref, layer_ref, ggrad_ref, igrad_ref):
    out_rows = rows_ref[:, 0:CAP].reshape(ROWS, 8, 128).reshape(ROWS, D)
    in_rows = rows_ref[:, CAP : 2 * CAP].reshape(ROWS, 8, 128).reshape(ROWS, D)
    slot_row = lax.broadcasted_iota(jnp.int32, (ROWS, TOK), 0)
    picks = [slot_row == pos_ref[k : k + 1, :] for k in range(2)]
    cot = cot_ref[...].astype(F32)
    layer = jnp.zeros((TOK, D), F32)
    for k in range(2):
        got = dot_cols(picks[k].astype(F32).astype(BF16), out_rows)
        layer = layer + gate_ref[:, k : k + 1] * got
        ggrad_ref[:, k : k + 1] = jnp.sum(cot * got, axis=1, keepdims=True)
    layer_ref[...] = layer.astype(BF16)
    both = (picks[0] | picks[1]).astype(F32).astype(BF16)
    igrad_ref[...] = dot_cols(both, in_rows).astype(BF16)


def local(tokens, gate_values, expert_ids, cotangent, weight_in, weight_out):
    tok_all = TOK * lax.axis_size("dp") * lax.axis_size("seq")
    factor = (E / (2.0 * tok_all)) ** 0.5
    shape = jax.ShapeDtypeStruct
    piece = (PIECES, 2, 128 // PIECES, FF // 2)
    dma = pltpu.SemaphoreType.DMA
    rows_shape = shape((E, 2 * CAP, 8, 128), BF16)
    big = pltpu.CompilerParams(vmem_limit_bytes=60 << 20)
    send, pos = pl.pallas_call(
        pick_kernel,
        out_shape=(rows_shape, shape((2, TOK), jnp.int32)),
        in_specs=[VMEM] * 4,
        out_specs=(VMEM, VMEM),
        compiler_params=big,
    )(expert_ids.T, gate_values.T, tokens, cotangent)
    rows, full_in, full_out = pl.pallas_call(
        gather_kernel,
        out_shape=(rows_shape, shape((FF, D), BF16), shape((FF, D), BF16)),
        in_specs=[VMEM] * 3,
        out_specs=(VMEM,) * 3,
        scratch_shapes=[
            pltpu.VMEM((2, 17, PAIR, D), BF16),
            dma((2,)), dma((E,)), dma((E,)),
            dma((2, PIECES, 17)), dma((2, PIECES, 17)), dma((2, 17)), dma((2, 16)),
        ],
        compiler_params=pltpu.CompilerParams(
            collective_id=0, has_side_effects=True, vmem_limit_bytes=60 << 20
        ),
    )(send, weight_in, weight_out)
    back, grads = pl.pallas_call(
        functools.partial(expert_kernel, factor),
        out_shape=(rows_shape, shape((2, 8) + piece, BF16)),
        in_specs=[VMEM] * 3,
        out_specs=(VMEM, VMEM),
        scratch_shapes=[
            pltpu.VMEM((ROWS, D), BF16), pltpu.VMEM((ROWS, D), BF16),
            pltpu.VMEM((ROWS, D), F32), pltpu.VMEM((ROWS, D), F32),
        ],
        compiler_params=big,
    )(rows, full_in, full_out)
    returned, grad_in, grad_out = pl.pallas_call(
        scatter_kernel,
        out_shape=(rows_shape, shape((64, FF // 2), F32), shape((64, FF // 2), F32)),
        in_specs=[VMEM] * 2,
        out_specs=(VMEM,) * 3,
        scratch_shapes=[
            pltpu.VMEM((17,) + piece, BF16),
            pltpu.VMEM((16,) + piece, BF16), pltpu.VMEM((16,) + piece, BF16),
            pltpu.VMEM((PIECES // 2,) + piece[1:], BF16),
            dma((E,)), dma((E,)), dma((PIECES, 16)), dma((PIECES, 17)),
            dma((PIECES, 16)), dma((PIECES, 16)), dma(()), dma(()),
        ],
        compiler_params=pltpu.CompilerParams(
            collective_id=1, has_side_effects=True, vmem_limit_bytes=60 << 20
        ),
    )(back, grads)
    layer_out, gate_grad, input_grad = pl.pallas_call(
        combine_kernel,
        out_shape=(shape((TOK, D), BF16), shape((TOK, 2), F32), shape((TOK, D), BF16)),
        in_specs=[VMEM] * 4,
        out_specs=(VMEM,) * 3,
        compiler_params=big,
    )(returned, pos, gate_values, cotangent)
    return layer_out, gate_grad, input_grad, grad_in, grad_out


def solution(mesh):
    tok = P(("dp", "seq"), None)
    return jax.shard_map(
        local,
        mesh=mesh,
        in_specs=(tok, tok, tok, tok, P("seq", None), P("seq", None)),
        out_specs=(tok, tok, tok, P("dp", "seq"), P("dp", "seq")),
        check_vma=False,
    )
```

```python
import functools

import jax
import jax.numpy as jnp
from jax import lax
from jax.experimental import pallas as pl
from jax.experimental.pallas import tpu as pltpu
from jax.sharding import PartitionSpec as P

MESH = pl.DeviceIdType.MESH
BF16 = jnp.bfloat16
F32 = jnp.float32

D = 1024
E = 32
FF = 1024
CAP = 9
TOK = 128
ROWS = E * CAP
PLANES = 32
PAIR = 64
PIECES = 4
AHEAD = 8
LAG = 0
WIN = 1
FCHUNK = 256

gelu_scale = 0.7978845608028654
gelu_cubic = 0.044715

VMEM = pl.BlockSpec(memory_space=pltpu.VMEM)


def plane_device(expert, plane):
    x = expert % 4
    y = (expert // 4 + x) % 4
    return {"dp": x % 2 * 8 + y * 2 + expert // 16 % 2, "seq": plane * 2 + x // 2}


def position():
    seq = lax.axis_index("seq")
    dp = lax.axis_index("dp")
    plane = seq // 2
    x_hi = seq % 2
    x = x_hi * 2 + dp // 8
    own = x + (dp // 2 % 4 - x + 4) % 4 * 4 + 16 * (dp % 2)
    return plane, x_hi, dp, own


def up_of(plane, x_hi):
    return {"seq": (plane + 1) % PLANES * 2 + x_hi}


def down_of(plane, x_hi):
    return {"seq": (plane + PLANES - 1) % PLANES * 2 + x_hi}


def enter(plane, x_hi, own):
    barrier = pltpu.get_barrier_semaphore()
    pl.semaphore_signal(barrier, inc=1, device_id=up_of(plane, x_hi), device_id_type=MESH)
    pl.semaphore_signal(barrier, inc=1, device_id=down_of(plane, x_hi), device_id_type=MESH)

    @pl.loop(1, E)
    def _(k):
        pl.semaphore_signal(
            barrier, inc=1, device_id=plane_device((own + k) % E, plane), device_id_type=MESH
        )

    def ready():
        pl.semaphore_wait(barrier, E + 1)

    return ready


def dot_t(a, b):
    return lax.dot_general(a, b, (((1,), (1,)), ((), ())), preferred_element_type=F32)


def dot_cols(a, b):
    return lax.dot_general(a, b, (((0,), (0,)), ((), ())), preferred_element_type=F32)


def pick_rows(ids_ref, gate_ref, tok_ref, cot_ref, send_ref, pos_ref):
    expert = lax.broadcasted_iota(jnp.int32, (E, TOK), 0)
    hot = [(expert == ids_ref[k : k + 1, :]).astype(F32) for k in range(2)]
    row = lax.broadcasted_iota(jnp.int32, (TOK, TOK), 0)
    col = lax.broadcasted_iota(jnp.int32, (TOK, TOK), 1)
    earlier = (row < col).astype(BF16)
    before = jnp.dot((hot[0] + hot[1]).astype(BF16), earlier, preferred_element_type=F32)
    slot_row = lax.broadcasted_iota(jnp.int32, (ROWS, TOK), 0)
    picks = []
    gates = jnp.zeros((ROWS, 1), F32)
    for k in range(2):
        slot = jnp.sum(before * hot[k], axis=0, keepdims=True).astype(jnp.int32)
        at = ids_ref[k : k + 1, :] * CAP + slot
        pos_ref[k : k + 1, :] = at
        pick = slot_row == at
        picks.append(pick)
        gates = gates + jnp.sum(
            jnp.where(pick, gate_ref[k : k + 1, :], 0.0), axis=1, keepdims=True
        )
    both = (picks[0] | picks[1]).astype(F32).astype(BF16)
    x_rows = jnp.dot(both, tok_ref[...], preferred_element_type=F32).astype(BF16)
    send_ref[:, 0:CAP] = x_rows.reshape(ROWS, 8, 128).reshape(E, CAP, 8, 128)
    d_rows = (jnp.dot(both, cot_ref[...], preferred_element_type=F32) * gates).astype(BF16)
    send_ref[:, CAP : 2 * CAP] = d_rows.reshape(ROWS, 8, 128).reshape(E, CAP, 8, 128)


def start_rows(plane, own, src, dst, ssem, rsem):
    keep = pltpu.make_async_copy(src.at[own], dst.at[own], ssem.at[0])
    keep.start()

    def copy(k):
        to = (own + k) % E
        return pltpu.make_async_remote_copy(
            src_ref=src.at[to],
            dst_ref=dst.at[own],
            send_sem=ssem.at[k],
            recv_sem=rsem.at[k],
            device_id=plane_device(to, plane),
            device_id_type=MESH,
        )

    @pl.loop(1, E)
    def _(k):
        copy(k).start()

    def finish():
        keep.wait()

        @pl.loop(1, E)
        def _(k):
            copy(k).wait()

    return finish


def gather_kernel(
    ids_ref, gate_ref, tok_ref, cot_ref, win_ref, wout_ref, rows_ref, fin_ref, fout_ref, pos_ref,
    send_ref, held, own_sem, tok_send, tok_recv, ring_send, ring_recv, host_send, host_recv,
):
    plane, x_hi, dp, own = position()
    core = dp % 2
    chip = x_hi * 8 + dp // 2
    steps = 16 - core
    toward = 1 - 2 * core
    onward = {"seq": (plane + toward + PLANES) % PLANES * 2 + x_hi}
    slab = pl.ds(pl.multiple_of(dp // 2 * PAIR, PAIR), PAIR)
    place = pl.ds(pl.multiple_of(chip * PAIR, PAIR), PAIR)
    full = (fin_ref, fout_ref)
    mine = [
        pltpu.make_async_copy(ref.at[slab], held.at[a, 0], own_sem.at[a])
        for a, ref in enumerate((win_ref, wout_ref))
    ]
    for c in mine:
        c.start()
    ready = enter(plane, x_hi, own)
    pick_rows(ids_ref, gate_ref, tok_ref, cot_ref, send_ref, pos_ref)
    for c in mine:
        c.wait()
    ready()
    cut = PAIR // PIECES

    def ring(a, h, step):
        return pltpu.make_async_remote_copy(
            src_ref=held.at[a, step - 1, pl.ds(h * cut, cut)],
            dst_ref=held.at[a, step, pl.ds(h * cut, cut)],
            send_sem=ring_send.at[a, h, step],
            recv_sem=ring_recv.at[a, h, step],
            device_id=onward,
            device_id_type=MESH,
        )

    def to_host(a, step):
        return pltpu.make_async_remote_copy(
            src_ref=held.at[a, step],
            dst_ref=full[a].at[place],
            send_sem=host_send.at[a, step],
            recv_sem=host_recv.at[a, chip],
            device_id=plane_device((plane - toward * step + 2 * PLANES) % PLANES, plane),
            device_id_type=MESH,
        )

    def is_own(step):
        return (plane - toward * step + 2 * PLANES) % PLANES == own

    def deliver(step):
        for a in range(2):
            @pl.when(is_own(step))
            def _():
                pltpu.make_async_copy(
                    held.at[a, step], full[a].at[place], host_recv.at[a, chip]
                ).start()

            @pl.when(~is_own(step))
            def _():
                to_host(a, step).start()

    for h in range(PIECES):
        for a in range(2):
            ring(a, h, 1).start()

    @pl.when(core == 1)
    def _():
        deliver(0)

    finish_rows = start_rows(plane, own, send_ref, rows_ref, tok_send, tok_recv)

    @pl.loop(1, 17)
    def _(step):
        @pl.when(step <= steps)
        def _():
            for h in range(PIECES):
                for a in range(2):
                    ring(a, h, step).wait_recv()

                    @pl.when(step < steps)
                    def _():
                        ring(a, h, step + 1).start()

        @pl.when(step % WIN == 0)
        def _():
            @pl.loop(0, WIN)
            def _(i):
                at = step - WIN + 1 + (i + own) % WIN

                @pl.when(at <= steps)
                def _():
                    deliver(at)

    finish_rows()

    @pl.loop(1, 17)
    def _(step):
        @pl.when(step <= steps)
        def _():
            for a in range(2):
                for h in range(PIECES):
                    ring(a, h, step).wait_send()

    @pl.loop(0, 17)
    def _(step):
        for a in range(2):
            @pl.when((step <= steps) & ((step > 0) | (core == 1)) & ~is_own(step))
            def _():
                to_host(a, step).wait_send()

    @pl.loop(0, 16)
    def _(c):
        there = pl.ds(pl.multiple_of(c * PAIR, PAIR), PAIR)
        for a in range(2):
            pltpu.make_async_copy(held.at[a, 0], full[a].at[there], host_recv.at[a, c]).wait()


def work_expert(factor, rows_ref, fin_ref, fout_ref, back_ref, grad_ref, x, d, xt, dt, out, inp):
    x[...] = rows_ref[:, 0:CAP].reshape(ROWS, 8, 128).reshape(ROWS, D)
    d[...] = rows_ref[:, CAP : 2 * CAP].reshape(ROWS, 8, 128).reshape(ROWS, D)
    xt[...] = x[...].T
    dt[...] = d[...].T
    out[...] = jnp.zeros_like(out)
    inp[...] = jnp.zeros_like(inp)

    @pl.loop(0, FF // FCHUNK)
    def _(c):
        units = pl.ds(pl.multiple_of(c * FCHUNK, FCHUNK), FCHUNK)
        wi = fin_ref[units, :]
        wo = fout_ref[units, :]
        v = dot_t(x[...], wi)
        t = jnp.tanh(gelu_scale * (v + gelu_cubic * v * v * v))
        act = (0.5 * v * (1.0 + t)).astype(BF16)
        slope = 0.5 * (1.0 + t) + 0.5 * v * (1.0 - t * t) * gelu_scale * (
            1.0 + 3.0 * gelu_cubic * v * v
        )
        dhid = (dot_t(d[...], wo) * slope).astype(BF16)
        out[...] += jnp.dot(act, wo, preferred_element_type=F32)
        inp[...] += jnp.dot(dhid, wi, preferred_element_type=F32)
        cols = pl.ds(pl.multiple_of(c % 2 * FCHUNK, FCHUNK), FCHUNK)
        g_in = (jnp.dot(xt[...], dhid, preferred_element_type=F32) * factor).astype(BF16)
        grad_ref[c // 2, :, :, 0, :, cols] = g_in.reshape(8, PIECES, 128 // PIECES, FCHUNK)
        g_out = (jnp.dot(dt[...], act, preferred_element_type=F32) * factor).astype(BF16)
        grad_ref[c // 2, :, :, 1, :, cols] = g_out.reshape(8, PIECES, 128 // PIECES, FCHUNK)

    back_ref[:, 0:CAP] = out[...].astype(BF16).reshape(ROWS, 8, 128).reshape(E, CAP, 8, 128)
    back_ref[:, CAP : 2 * CAP] = inp[...].astype(BF16).reshape(ROWS, 8, 128).reshape(E, CAP, 8, 128)


def scatter_kernel(
    factor, in_ref, fin_ref, fout_ref, rows_ref, sum_ref,
    back_ref, grad_ref, x, d, xt, dt, out, inp, parts, got, held, other,
    tok_send, tok_recv, part_send, part_recv, ring_send, ring_recv, swap_send, swap_recv,
):
    plane, x_hi, dp, own = position()
    core = dp % 2
    chip = x_hi * 8 + dp // 2
    steps = 16 - core
    toward = 1 - 2 * core
    onward = {"seq": (plane + toward + PLANES) % PLANES * 2 + x_hi}
    cut = 2 * 64 // PIECES
    ready = enter(plane, x_hi, own)
    work_expert(factor, in_ref, fin_ref, fout_ref, back_ref, grad_ref, x, d, xt, dt, out, inp)
    ready()

    at_up = (plane + 16 - own + PLANES) % PLANES
    goes_down = at_up // 17
    my_step = at_up + goes_down * (31 - 2 * at_up)

    def part(k, h):
        to = (chip + k) % 16
        return pltpu.make_async_remote_copy(
            src_ref=grad_ref.at[to // 8, to % 8, h],
            dst_ref=parts.at[my_step, h],
            send_sem=part_send.at[h, k],
            recv_sem=part_recv.at[h, my_step],
            device_id={"dp": to % 8 * 2 + goes_down, "seq": plane * 2 + to // 8},
            device_id_type=MESH,
        )

    def send_parts():
        @pl.loop(0, PIECES)
        def _(h):
            @pl.when(goes_down == core)
            def _():
                pltpu.make_async_copy(
                    grad_ref.at[x_hi, dp // 2, h], parts.at[my_step, h], part_recv.at[h, my_step]
                ).start()

            @pl.when(goes_down != core)
            def _():
                part(0, h).start()

            @pl.loop(1, 16)
            def _(k):
                part(k, h).start()

    def await_part(step, h):
        pltpu.make_async_copy(
            grad_ref.at[x_hi, dp // 2, h], parts.at[step, h], part_recv.at[h, step]
        ).wait()

    def ring(h, step, first=False):
        return pltpu.make_async_remote_copy(
            src_ref=parts.at[0, h] if first else held.at[step, h],
            dst_ref=got.at[step, h],
            send_sem=ring_send.at[h, step],
            recv_sem=ring_recv.at[h, step],
            device_id=onward,
            device_id_type=MESH,
        )

    @pl.when(my_step < AHEAD)
    def _():
        send_parts()

    finish_rows = start_rows(plane, own, back_ref, rows_ref, tok_send, tok_recv)

    @pl.loop(0, 16 + LAG * (PIECES - 1))
    def _(tick):
        @pl.when(my_step == tick + AHEAD)
        def _():
            send_parts()

        for h in range(PIECES):
            t = tick - LAG * h

            @pl.when(t == 0)
            def _():
                await_part(0, h)
                ring(h, 0, True).start()

            @pl.when((t > 0) & (t < steps))
            def _():
                await_part(t, h)
                ring(h, t - 1).wait_recv()
                held[t, h] = (got[t - 1, h].astype(F32) + parts[t, h].astype(F32)).astype(BF16)
                ring(h, t).start()

    @pl.when(my_step >= 16 + LAG * (PIECES - 1) + AHEAD)
    def _():
        send_parts()

    for h in range(PIECES):
        ring(h, steps - 1).wait_recv()

        @pl.when(core == 0)
        def _():
            await_part(16, h)
            held[0, h] = (got[15, h].astype(F32) + parts[16, h].astype(F32)).astype(BF16)

        @pl.when(core == 1)
        def _():
            held[0, h] = got[14, h]

    half = PIECES // 2
    mine = pl.ds(core * half, half)
    theirs = pl.ds(half - core * half, half)
    swap = pltpu.make_async_remote_copy(
        src_ref=held.at[0, theirs],
        dst_ref=other,
        send_sem=swap_send,
        recv_sem=swap_recv,
        device_id={"dp": dp + 1 - 2 * core},
        device_id_type=MESH,
    )
    swap.start()
    swap.wait()
    sum_ref[...] = held[0, mine].astype(F32) + other[...].astype(F32)
    finish_rows()

    @pl.loop(0, PIECES)
    def _(h):
        @pl.when(goes_down != core)
        def _():
            part(0, h).wait_send()

        @pl.loop(1, 16)
        def _(k):
            part(k, h).wait_send()

    for h in range(PIECES):
        ring(h, 0, True).wait_send()

    @pl.loop(1, 16)
    def _(t):
        @pl.when(t < steps)
        def _():
            for h in range(PIECES):
                ring(h, t).wait_send()


def combine_kernel(
    rows_ref, sum_ref, pos_ref, gate_ref, cot_ref, layer_ref, ggrad_ref, igrad_ref, gin_ref, gout_ref
):
    for a, ref in enumerate((gin_ref, gout_ref)):
        ref[...] = sum_ref[:, a].reshape(64, FF // 2)
    out_rows = rows_ref[:, 0:CAP].reshape(ROWS, 8, 128).reshape(ROWS, D)
    in_rows = rows_ref[:, CAP : 2 * CAP].reshape(ROWS, 8, 128).reshape(ROWS, D)
    slot_row = lax.broadcasted_iota(jnp.int32, (ROWS, TOK), 0)
    picks = [slot_row == pos_ref[k : k + 1, :] for k in range(2)]
    cot = cot_ref[...].astype(F32)
    layer = jnp.zeros((TOK, D), F32)
    gates = gate_ref[...].T
    dots = []
    for k in range(2):
        got = dot_cols(picks[k].astype(F32).astype(BF16), out_rows)
        layer = layer + gates[:, k : k + 1] * got
        dots.append(jnp.sum(cot * got, axis=1, keepdims=True))
    ggrad_ref[...] = jnp.concatenate(dots, axis=1).T
    layer_ref[...] = layer.astype(BF16)
    both = (picks[0] | picks[1]).astype(F32).astype(BF16)
    igrad_ref[...] = dot_cols(both, in_rows).astype(BF16)


def local(tokens, gate_values, expert_ids, cotangent, weight_in, weight_out):
    tok_all = TOK * lax.axis_size("dp") * lax.axis_size("seq")
    factor = (E / (2.0 * tok_all)) ** 0.5
    shape = jax.ShapeDtypeStruct
    piece = (PIECES, 2, 128 // PIECES, FF // 2)
    dma = pltpu.SemaphoreType.DMA
    rows_shape = shape((E, 2 * CAP, 8, 128), BF16)
    big = pltpu.CompilerParams(vmem_limit_bytes=60 << 20)
    rows, full_in, full_out, pos = pl.pallas_call(
        gather_kernel,
        out_shape=(
            rows_shape, shape((FF, D), BF16), shape((FF, D), BF16), shape((2, TOK), jnp.int32)
        ),
        in_specs=[VMEM] * 6,
        out_specs=(VMEM,) * 4,
        scratch_shapes=[
            pltpu.VMEM(rows_shape.shape, BF16),
            pltpu.VMEM((2, 17, PAIR, D), BF16),
            dma((2,)), dma((E,)), dma((E,)),
            dma((2, PIECES, 17)), dma((2, PIECES, 17)), dma((2, 17)), dma((2, 16)),
        ],
        compiler_params=pltpu.CompilerParams(
            collective_id=0, has_side_effects=True, vmem_limit_bytes=60 << 20
        ),
    )(expert_ids.T, gate_values.T, tokens, cotangent, weight_in, weight_out)
    sums = (PIECES // 2,) + piece[1:]
    returned, grads = pl.pallas_call(
        functools.partial(scatter_kernel, factor),
        out_shape=(rows_shape, shape(sums, F32)),
        in_specs=[VMEM] * 3,
        out_specs=(VMEM,) * 2,
        scratch_shapes=[
            pltpu.VMEM(rows_shape.shape, BF16), pltpu.VMEM((2, 8) + piece, BF16),
            pltpu.VMEM((ROWS, D), BF16), pltpu.VMEM((ROWS, D), BF16),
            pltpu.VMEM((D, ROWS), BF16), pltpu.VMEM((D, ROWS), BF16),
            pltpu.VMEM((ROWS, D), F32), pltpu.VMEM((ROWS, D), F32),
            pltpu.VMEM((17,) + piece, BF16),
            pltpu.VMEM((16,) + piece, BF16), pltpu.VMEM((16,) + piece, BF16),
            pltpu.VMEM(sums, BF16),
            dma((E,)), dma((E,)), dma((PIECES, 16)), dma((PIECES, 17)),
            dma((PIECES, 16)), dma((PIECES, 16)), dma(()), dma(()),
        ],
        compiler_params=pltpu.CompilerParams(
            collective_id=1, has_side_effects=True, vmem_limit_bytes=60 << 20
        ),
    )(rows, full_in, full_out)
    layer_out, gate_grad, input_grad, grad_in, grad_out = pl.pallas_call(
        combine_kernel,
        out_shape=(
            shape((TOK, D), BF16), shape((2, TOK), F32), shape((TOK, D), BF16),
            shape((64, FF // 2), F32), shape((64, FF // 2), F32),
        ),
        in_specs=[VMEM] * 5,
        out_specs=(VMEM,) * 5,
        compiler_params=big,
    )(returned, grads, pos, gate_values.T, cotangent)
    return layer_out, gate_grad.T, input_grad, grad_in, grad_out


def solution(mesh):
    tok = P(("dp", "seq"), None)
    return jax.shard_map(
        local,
        mesh=mesh,
        in_specs=(tok, tok, tok, tok, P("seq", None), P("seq", None)),
        out_specs=(tok, tok, tok, P("dp", "seq"), P("dp", "seq")),
        check_vma=False,
    )
```
